256 devices in a mesh: section: 8 (over y_lo, x), dp: 32 (over y_hi, z, core).
Axes of the slice: x: 4, y: 4 (y_hi: 2, y_lo: 2; y = y_hi * 2 + y_lo), z: 8, core: 2. Of those that a mesh axis runs over, the one named last changes fastest.
Arguments:
- nbr_embed: bfloat16 [32, 4, 128, 896], P('dp', None, 'section'), may hold values from -140 to 140
- enc_weight: bfloat16 [896, 896], replicated, may hold values from -0.1875 to 0.1875
- enc_gain: float32 [896], replicated, may hold values from 0.1 to 1.9
- kv_weight: bfloat16 [8, 4096, 896], P('section'), may hold values from -0.1875 to 0.1875
- queries: bfloat16 [8, 4096, 2048], P('section', 'dp'), may hold values from -6 to 6
- pos_bias: bfloat16 [8, 16, 64, 256], P('section'), may hold values from -8 to 240
- nbr_ids: int32 [32, 2, 2], P('dp'), may hold values from 0 to 3
- ctx_grad: bfloat16 [8, 4096, 2048], P('section', 'dp'), may hold values from -12 to 12
Outputs:
- q_grad: bfloat16 [8, 4096, 2048], P('section', 'dp')
- kv_weight_grad: float32 [8, 4096, 896], P('section', 'dp')
- enc_weight_grad: float32 [896, 896], P('section')
- enc_gain_grad: float32 [896], replicated
- embed_grad: bfloat16 [32, 4, 128, 896], P('dp', None, 'section')
The draws below stay inside these ranges and needn't reach their ends.
All inputs are finite; a program needn't handle non-finite values.
Results may differ from the reference program's by a relative error of at most 0.02.
Values may be sent and summed in bfloat16 or wider, within the bound.
A program may use at most 128 MiB of HBM per device.

```python
import math
import jax
import jax.numpy as jnp
from jax import lax

HEADS = 16
HEAD = 128
ENC_D = 896
BLOCK = 64
NBR = 2
NLEN = 128
TOK_DEV = 128
NSET = 4
TOKENS = 4096
N_SECTION = 8
N_DP = 32


def draw_nbr_embed(key, part):
    full_shape = (N_DP, NSET, NLEN, ENC_D)
    keys_list = jax.random.split(key, 3)
    col_scale = jnp.exp(jax.random.uniform(keys_list[2], (1, 1, 1, ENC_D), jnp.float32, -0.5 * math.log(10.0), 0.5 * math.log(10.0)))
    row_scale = jnp.exp(jax.random.uniform(keys_list[1], (N_DP, NSET, NLEN, 1), jnp.float32, 0.0, math.log(10.0)))
    base_vals = jnp.clip(jax.random.normal(keys_list[0], full_shape, jnp.float32), -4.0, 4.0)
    return (base_vals * row_scale * col_scale).astype(jnp.bfloat16)


def draw_pos_bias(key, part):
    key_rows = NBR * NLEN
    full_shape = (N_SECTION, HEADS, BLOCK, key_rows)
    keys_list = jax.random.split(key, 1)
    result = jnp.clip(jax.random.normal(keys_list[0], full_shape, jnp.float32), -6.0, 6.0)
    return result.astype(jnp.bfloat16)


def plant(drawn, stream_key, low, top_value):
    longest = drawn.shape.index(max(drawn.shape))
    spots = []
    for shift in (0, 1):
        where = [jax.random.randint(jax.random.fold_in(stream_key, axis), (), 0, length) for axis, length in enumerate(drawn.shape)]
        where[longest] = (where[longest] + shift) % drawn.shape[longest]
        spots.append(tuple(where))
    return drawn.at[spots[0]].set(low).at[spots[1]].set(top_value)


def block_levels(own_key, extent, cuts, low, top_value):
    loudness = 1.0
    for axis_at, blocks in cuts:
        heights = jax.random.uniform(jax.random.fold_in(jax.random.fold_in(own_key, 6), axis_at), (blocks,), jnp.float32, low / len(cuts), top_value / len(cuts))
        loudness = loudness * jnp.repeat(jnp.exp(heights), extent[axis_at] // blocks).reshape((-1,) + (1,) * (len(extent) - 1 - axis_at))
    return loudness


def scatter_about(rng, extent, spread, reach, cuts=(), kind=jnp.bfloat16):
    values = jax.random.normal(rng, extent, jnp.float32) * spread
    if len(cuts) > 0:
        values = block_levels(rng, extent, cuts, -0.22, 0.18) * values
    return jnp.clip(values, min=-reach, max=reach).astype(kind)


def setup_inputs(seed: int = 0) -> dict:
    keys = jax.random.split(jax.random.key(seed), 9)
    return {
        "nbr_embed": draw_nbr_embed(jax.random.fold_in(keys[8], 71), 0),
        "enc_weight": scatter_about(keys[1], (ENC_D, ENC_D), ENC_D ** -0.5, 0.1875),
        "enc_gain": jnp.clip(1.0 + 0.18 * jax.random.normal(keys[2], (ENC_D,), jnp.float32), 0.1, 1.9),
        "kv_weight": scatter_about(keys[3], (N_SECTION, 2 * HEADS * HEAD, ENC_D), ENC_D ** -0.5, 0.1875, ((0, 8),)),
        "queries": scatter_about(keys[4], (N_SECTION, TOKENS, HEADS * HEAD), 1.0, 6.0, ((0, 8), (1, 32))),
        "pos_bias": draw_pos_bias(jax.random.fold_in(keys[8], 71), 0),
        "nbr_ids": plant(jax.random.randint(keys[6], (N_DP, TOK_DEV // BLOCK, NBR), 0, NSET), jax.random.fold_in(keys[6], 1), 0, NSET - 1).astype(jnp.int32),
        "ctx_grad": scatter_about(keys[7], (N_SECTION, TOKENS, HEADS * HEAD), 2.0, 12.0, ((0, 8), (1, 32))),
    }


eps_norm = 1e-06

def replica_layer(weights, query_blk, bias_blk, ids_blk, grad_blk, encoded_rows):
    head_width = HEADS * HEAD
    key_rows = NBR * NLEN
    blocks = TOK_DEV // BLOCK
    factor = 1.0 / math.sqrt(HEAD)
    projected = lax.dot_general(encoded_rows, weights, (((1,), (1,)), ((), ())), preferred_element_type=jnp.float32).astype(jnp.bfloat16)
    projected = projected.reshape(NSET, NLEN, 2 * head_width)
    selector = (ids_blk[:, :, None] == jnp.arange(NSET, dtype=jnp.int32)[None, None, :]).astype(jnp.float32)
    chosen = jnp.einsum('cne,eld->cnld', selector, projected.astype(jnp.float32)).astype(jnp.bfloat16)
    chosen = chosen.reshape(blocks, key_rows, 2 * head_width)
    keys_all = chosen[:, :, :head_width].reshape(blocks, key_rows, HEADS, HEAD).astype(jnp.float32)
    values_all = chosen[:, :, head_width:].reshape(blocks, key_rows, HEADS, HEAD).astype(jnp.float32)
    query_all = query_blk.reshape(blocks, BLOCK, HEADS, HEAD).astype(jnp.float32)
    upstream = grad_blk.reshape(blocks, BLOCK, HEADS, HEAD).astype(jnp.float32)
    scores = jnp.einsum('cqhd,ckhd->chqk', query_all, keys_all) * factor + bias_blk.astype(jnp.float32)[None]
    row_peak = lax.optimization_barrier(jnp.max(scores, axis=-1, keepdims=True))
    exp_scores = jnp.exp(scores - row_peak)
    attn_probs = exp_scores / lax.optimization_barrier(jnp.sum(exp_scores, axis=-1, keepdims=True))
    probs_low = attn_probs.astype(jnp.bfloat16)
    grad_probs = jnp.einsum('cqhd,ckhd->chqk', upstream, values_all)
    row_inner = lax.optimization_barrier(jnp.sum(attn_probs * grad_probs, axis=-1, keepdims=True))
    grad_scores = (attn_probs * (grad_probs - row_inner)).astype(jnp.bfloat16).astype(jnp.float32)
    grad_query = (jnp.einsum('chqk,ckhd->cqhd', grad_scores, keys_all) * factor).astype(jnp.bfloat16)
    grad_query = grad_query.reshape(TOK_DEV, head_width)
    grad_keys = jnp.einsum('chqk,cqhd->ckhd', grad_scores, query_all) * factor
    grad_values = jnp.einsum('chqk,cqhd->ckhd', probs_low.astype(jnp.float32), upstream)
    grad_chosen = jnp.concatenate([grad_keys.reshape(blocks, key_rows, head_width), grad_values.reshape(blocks, key_rows, head_width)], axis=-1)
    grad_chosen = grad_chosen.reshape(blocks, NBR, NLEN, 2 * head_width)
    grad_set = jnp.einsum('cne,cnld->eld', selector, grad_chosen).astype(jnp.bfloat16)
    grad_set = grad_set.reshape(NSET * NLEN, 2 * head_width)
    grad_weights = lax.dot_general(grad_set, encoded_rows, (((0,), (0,)), ((), ())), preferred_element_type=jnp.float32)
    grad_weights = lax.optimization_barrier(grad_weights.astype(jnp.bfloat16)).astype(jnp.float32)
    grad_encoded = jnp.dot(grad_set, weights, preferred_element_type=jnp.float32)
    return (grad_query, grad_weights, grad_encoded)

def reference(nbr_embed, enc_weight, enc_gain, kv_weight, queries, pos_bias, nbr_ids, ctx_grad):
    head_width = HEADS * HEAD
    flat_rows = nbr_embed.reshape(N_DP * NSET * NLEN, ENC_D)
    mixed_rows = flat_rows.astype(jnp.float32) + jnp.dot(flat_rows, enc_weight, preferred_element_type=jnp.float32)
    inverse = lax.rsqrt(lax.optimization_barrier(jnp.mean(mixed_rows * mixed_rows, axis=-1, keepdims=True)) + eps_norm)
    normed = mixed_rows * inverse
    encoded = (normed * enc_gain[None, :]).astype(jnp.bfloat16).reshape(N_DP, NSET * NLEN, ENC_D)
    query_rep = queries.reshape(N_SECTION, N_DP, TOK_DEV, head_width)
    grad_rep = ctx_grad.reshape(N_SECTION, N_DP, TOK_DEV, head_width)

    def section_step(grad_total, section_inputs):
        weights, query_section, bias_section, grad_section = section_inputs

        def replica_step(running, replica_inputs):
            query_blk, ids_blk, grad_blk, encoded_rows = replica_inputs
            grad_query, grad_weights, grad_encoded = replica_layer(weights, query_blk, bias_section, ids_blk, grad_blk, encoded_rows)
            return (running + grad_weights, (grad_query, grad_encoded))
        zero_weights = jnp.zeros((2 * head_width, ENC_D), jnp.float32)
        weight_sum, (query_grads, encoded_grads) = lax.scan(replica_step, zero_weights, (query_section, nbr_ids, grad_section, encoded))
        return (grad_total + encoded_grads, (query_grads, weight_sum))
    zero_grad = jnp.zeros((N_DP, NSET * NLEN, ENC_D), jnp.float32)
    grad_encoded, (query_grads, kv_grads) = lax.scan(section_step, zero_grad, (kv_weight, query_rep, pos_bias, grad_rep))
    q_grad = query_grads.reshape(N_SECTION, N_DP * TOK_DEV, head_width)
    grad_flat = grad_encoded.reshape(N_DP * NSET * NLEN, ENC_D)
    gain_grad = lax.optimization_barrier(jnp.sum(grad_flat * normed, axis=0))
    grad_normed = grad_flat * enc_gain[None, :]
    grad_mixed = inverse * (grad_normed - normed * lax.optimization_barrier(jnp.mean(grad_normed * normed, axis=-1, keepdims=True)))
    grad_low = grad_mixed.astype(jnp.bfloat16)
    embed_grad = grad_mixed + lax.dot_general(grad_low, enc_weight, (((1,), (1,)), ((), ())), preferred_element_type=jnp.float32)
    embed_grad = embed_grad.astype(jnp.bfloat16).reshape(N_DP, NSET, NLEN, ENC_D)
    weight_grad = lax.dot_general(flat_rows, grad_low, (((0,), (0,)), ((), ())), preferred_element_type=jnp.float32)
    return (q_grad, kv_grads, weight_grad, gain_grad, embed_grad)
```

```python
import math

import jax
import jax.numpy as jnp
from jax import lax
from jax.experimental import pallas as pl
from jax.experimental.pallas import tpu as pltpu
from jax.sharding import PartitionSpec as P

HEADS = 16
HEAD = 128
ENC_D = 896
BLOCK = 64
NBR = 2
NLEN = 128
TOK_DEV = 128
NSET = 4
ROWS = NSET * NLEN
N_SEC = 8
N_Z = 8
LOCAL = NLEN // N_SEC
OWN_ROWS = ENC_D // N_SEC
PIECE = 16
QUAD_COLS = 256
FACTOR = 1.0 / math.sqrt(HEAD)
MESH = pl.DeviceIdType.MESH

eps_norm = 1e-06

VMEM_SPEC = pl.BlockSpec(memory_space=pltpu.VMEM)


def greet(peers):
    barrier = pltpu.get_barrier_semaphore()
    for peer in peers:
        pl.semaphore_signal(barrier, inc=1, device_id=peer, device_id_type=MESH)
    pl.semaphore_wait(barrier, len(peers))


def remote(src, dst, send_sem, recv_sem, peer):
    return pltpu.make_async_remote_copy(
        src_ref=src,
        dst_ref=dst,
        send_sem=send_sem,
        recv_sem=recv_sem,
        device_id=peer,
        device_id_type=MESH,
    )


def section_ids(me):
    y, x = me // 4, lax.rem(me, 4)
    steps = [(1, 0), (0, 1), (0, 3), (1, 1), (1, 3), (0, 2), (1, 2)]
    return [lax.rem(y + a, 2) * 4 + lax.rem(x + b, 4) for a, b in steps]


def section_sources(me):
    y, x = me // 4, lax.rem(me, 4)
    steps = [(1, 0), (0, 3), (0, 1), (1, 3), (1, 1), (0, 2), (1, 2)]
    return [lax.rem(y + a, 2) * 4 + lax.rem(x + b, 4) for a, b in steps]


def row_slot(index):
    return pl.ds(pl.multiple_of(index * LOCAL, LOCAL), LOCAL)


def dot_nt(a, b):
    return lax.dot_general(a, b, (((1,), (1,)), ((), ())), preferred_element_type=jnp.float32)


def dot_tn(a, b):
    return lax.dot_general(a, b, (((0,), (0,)), ((), ())), preferred_element_type=jnp.float32)


def dot_nn(a, b):
    return jnp.dot(a, b, preferred_element_type=jnp.float32)


def encode(x, enc_weight):
    mixed = x.astype(jnp.float32) + dot_nn(x, enc_weight)
    inverse = lax.rsqrt(jnp.mean(mixed * mixed, axis=-1, keepdims=True) + eps_norm)
    return mixed * inverse, inverse


def f32(x):
    return x.astype(jnp.float32)


def low(x):
    return x.astype(jnp.bfloat16)


def train_kernel(
    ids_ref,
    x_ref,
    gain_ref,
    encw_hbm,
    w_hbm,
    q_hbm,
    bias_hbm,
    g_hbm,
    qg_ref,
    kvg_ref,
    wg_ref,
    gg_ref,
    eg_ref,
    encw_ref,
    w_ref,
    q_ref,
    bias_ref,
    g_ref,
    x_all,
    enc_ref,
    xt_ref,
    gs_ref,
    dw_ref,
    core_recv,
    first_ref,
    plus_recv,
    minus_recv,
    fin_ref,
    y_recv,
    de_ref,
    de_recv,
    low_all,
    low_loc,
    gain_all,
    gain_loc,
    wp_ref,
    quad_recv,
    zp_ref,
    z_recv,
    za_ref,
    za_all,
    wa_all,
    load_sem,
    x_send,
    x_rsem,
    core_send,
    core_rsem,
    ring_send,
    ring_rsem,
    y_send,
    y_rsem,
    sec_send,
    sec_rsem,
    low_send,
    low_rsem,
    gn_send,
    gn_rsem,
    quad_send,
    quad_rsem,
    z_send,
    z_rsem,
    za_send,
    za_rsem,
    wa_send,
    wa_rsem,
):
    me = lax.axis_index("section")
    dp = lax.axis_index("dp")
    core = lax.rem(dp, 2)
    zed = lax.rem(dp // 2, N_Z)
    yhi = dp // (2 * N_Z)

    loads = [
        pltpu.make_async_copy(encw_hbm, encw_ref, load_sem.at[0]),
        pltpu.make_async_copy(w_hbm.at[0], w_ref, load_sem.at[1]),
        pltpu.make_async_copy(q_hbm.at[0], q_ref, load_sem.at[2]),
        pltpu.make_async_copy(bias_hbm.at[0], bias_ref, load_sem.at[3]),
        pltpu.make_async_copy(g_hbm.at[0], g_ref, load_sem.at[4]),
    ]
    for copy in loads:
        copy.start()

    def dp_peer(y, z, c):
        return {"dp": (y * N_Z + z) * 2 + c}

    targets = section_ids(me)
    sources = section_sources(me)
    sec = [{"section": t} for t in targets]
    z_peers = [dp_peer(yhi, lax.rem(zed + d, N_Z), core) for d in range(1, N_Z)]
    z_next, z_prev = z_peers[0], z_peers[N_Z - 2]
    core_peer = dp_peer(yhi, zed, 1 - core)
    y_peer = dp_peer(1 - yhi, zed, core)
    quad = [core_peer, y_peer, dp_peer(1 - yhi, zed, 1 - core)]
    greet(sec + z_peers + quad)

    x_copies = []
    for i, peer in enumerate(sec):
        copy = remote(x_ref, x_all.at[:, row_slot(me), :], x_send.at[i], x_rsem.at[i], peer)
        copy.start()
        x_copies.append(copy)
    x_all[:, row_slot(me), :] = x_ref[...]
    loads[0].wait()

    def encode_slots(slots):
        x = jnp.concatenate(
            [x_all[:, row_slot(s), :].reshape(NSET * LOCAL, ENC_D) for s in slots], axis=0
        )
        normed, _ = encode(x, encw_ref[...])
        encoded = low(normed * gain_ref[...])
        for n, s in enumerate(slots):
            enc_ref[:, row_slot(s), :] = encoded[
                n * NSET * LOCAL : (n + 1) * NSET * LOCAL
            ].reshape(NSET, LOCAL, ENC_D)

    for i in range(3):
        x_copies[i].wait_recv()
    encode_slots([me] + sources[:3])
    for i in range(3, 7):
        x_copies[i].wait_recv()
    encode_slots(sources[3:])
    for copy in loads[1:]:
        copy.wait()

    def picked(n, parts):
        chosen = parts[NSET - 1]
        for e in range(NSET - 2, -1, -1):
            chosen = jnp.where(ids_ref[n : n + 1, :] == e, parts[e], chosen)
        return chosen

    def core_z(i):
        half = (i + 1) // 2
        return lax.rem(zed + 4 + half * (1 - 2 * lax.rem(i, 2)), N_Z)

    def core_copy(i):
        z = core_z(i)
        return remote(
            dw_ref.at[1 - core, z], core_recv.at[z], core_send.at[i], core_rsem.at[i], core_peer
        )

    def chip_sum(z, y):
        return f32(dw_ref[core, z, y]) + f32(core_recv[z, y])

    def ring_copies(s):
        if s == 0:
            pairs = (
                (first_ref.at[0], plus_recv.at[0, 0], z_next),
                (first_ref.at[1], minus_recv.at[0, 1], z_prev),
            )
        else:
            pairs = (
                (plus_recv.at[s - 1], plus_recv.at[s], z_next),
                (minus_recv.at[s - 1], minus_recv.at[s], z_prev),
            )
        return [
            remote(src, dst, ring_send.at[s, n], ring_rsem.at[s, n], peer)
            for n, (src, dst, peer) in enumerate(pairs)
        ]

    def ring_step(s):
        zp = lax.rem(zed + 4 - s, N_Z)
        zm = lax.rem(zed + 4 + s, N_Z)
        copies = ring_copies(s)
        if s == 0:
            core_copy(0).wait_recv()
            for y in range(2):
                first_ref[y] = low(chip_sum(zp, y))
                copies[y].start()
            return
        earlier = ring_copies(s - 1)
        core_copy(2 * s - 1).wait_recv()
        earlier[0].wait_recv()
        for y in range(2):
            value = chip_sum(zp, y)
            if s > 1 or y == 0:
                value = value + f32(plus_recv[s - 1, y])
            plus_recv[s - 1, y] = low(value)
        copies[0].start()
        core_copy(2 * s).wait_recv()
        earlier[1].wait_recv()
        for y in range(2):
            value = chip_sum(zm, y)
            if s > 1 or y == 1:
                value = value + f32(minus_recv[s - 1, y])
            minus_recv[s - 1, y] = low(value)
        copies[1].start()

    def pair(i, carry):
        z = core_z(i)
        cols = pl.ds(pl.multiple_of(z * 2 * HEAD, 2 * HEAD), 2 * HEAD)
        vcols = pl.ds(
            pl.multiple_of(HEADS * HEAD + z * 2 * HEAD, 2 * HEAD), 2 * HEAD
        )
        enc = enc_ref[...].reshape(ROWS, ENC_D)
        keys = low(dot_nt(enc, w_ref[cols, :]))
        vals = low(dot_nt(enc, w_ref[vcols, :]))
        q2, g2 = q_ref[:, cols], g_ref[:, cols]
        dks, dvs, dkts, dvts, dqs = [], [], [], [], []
        heads = []
        for a in range(2):
            span = slice(a * HEAD, (a + 1) * HEAD)
            s_all = dot_nt(keys[:, span], q2[:, span])
            dp_all = dot_nt(vals[:, span], g2[:, span])
            b = f32(bias_ref[2 * z + a])
            heads.append((jnp.concatenate([b, b], axis=0).T, span, s_all, dp_all))
        for bias, span, s_all, dp_all in heads:
            q, g, k = q2[:, span], g2[:, span], keys[:, span]
            s_sets = [s_all[e * NLEN : (e + 1) * NLEN] for e in range(NSET)]
            dp_sets = [dp_all[e * NLEN : (e + 1) * NLEN] for e in range(NSET)]
            scores = [
                picked(n, s_sets) * FACTOR + bias[n * NLEN : (n + 1) * NLEN]
                for n in range(NBR)
            ]
            dprobs = [picked(n, dp_sets) for n in range(NBR)]
            peak = jnp.max(jnp.maximum(scores[0], scores[1]), axis=0, keepdims=True)
            ex = [jnp.exp(s - peak) for s in scores]
            share = 1.0 / jnp.sum(ex[0] + ex[1], axis=0, keepdims=True)
            p = [e * share for e in ex]
            inner = jnp.sum(p[0] * dprobs[0] + p[1] * dprobs[1], axis=0, keepdims=True)
            ds = [f32(low(p[n] * (dprobs[n] - inner))) for n in range(NBR)]
            pb = [f32(low(p[n])) for n in range(NBR)]
            zero = jnp.zeros_like(ds[0])
            ds_t, p_t = [], []
            for e in range(NSET):
                hit = [ids_ref[n : n + 1, :] == e for n in range(NBR)]
                ds_t.append(low(jnp.where(hit[0], ds[0], zero) + jnp.where(hit[1], ds[1], zero)))
                p_t.append(low(jnp.where(hit[0], pb[0], zero) + jnp.where(hit[1], pb[1], zero)))
            ds_t = jnp.concatenate(ds_t, axis=0)
            p_t = jnp.concatenate(p_t, axis=0)
            dks.append(low(dot_nn(ds_t, q) * FACTOR))
            dvs.append(low(dot_nn(p_t, g)))
            dkts.append(low(dot_nt(q.T, ds_t) * FACTOR))
            dvts.append(low(dot_nt(g.T, p_t)))
            dqs.append(low(dot_tn(ds_t, k) * FACTOR))
        qg_ref[0, :, cols] = jnp.concatenate(dqs, axis=1)
        gs_ref[:, cols] = jnp.concatenate(dks, axis=1)
        gs_ref[:, vcols] = jnp.concatenate(dvs, axis=1)
        dw = low(dot_nn(jnp.concatenate(dkts + dvts, axis=0), enc))
        for y in range(2):
            for c in range(2):
                at = (2 * y + c) * HEAD
                dw_ref[c, z, y] = dw[at : at + HEAD]
        core_copy(i).start()
        for s in range(4):

            @pl.when(i == 2 * s + 1)
            def _(s=s):
                ring_step(s)

        return carry

    lax.fori_loop(0, N_Z, pair, 0)

    sec_copies = []
    for half in range(2):
        rows = pl.ds(half * 2 * NLEN, 2 * NLEN)
        de_ref[2 * half : 2 * half + 2] = low(dot_nn(gs_ref[rows, :], w_ref[...])).reshape(
            2, NLEN, ENC_D
        )
        for i, peer in enumerate(sec):
            copy = remote(
                de_ref.at[2 * half : 2 * half + 2, row_slot(targets[i]), :],
                de_recv.at[i, 2 * half : 2 * half + 2],
                sec_send.at[half, i],
                sec_rsem.at[half, i],
                peer,
            )
            copy.start()
            sec_copies.append(copy)

    normed, inverse = encode(x_ref[...].reshape(NSET * LOCAL, ENC_D), encw_ref[...])
    xt_ref[...] = x_all[...].reshape(ROWS, ENC_D).T

    core_copy(N_Z - 1).wait_recv()
    for copy in ring_copies(3):
        copy.wait_recv()
    for y in range(2):
        fin_ref[y] = low(chip_sum(zed, y) + f32(plus_recv[3, y]) + f32(minus_recv[3, y]))
    y_copy = remote(fin_ref.at[1 - yhi], y_recv, y_send, y_rsem, y_peer)
    y_copy.start()

    for copy in sec_copies:
        copy.wait_recv()
    grad = f32(de_ref[:, row_slot(me), :])
    for i in range(N_SEC - 1):
        grad = grad + f32(de_recv[i])
    grad = grad.reshape(NSET * LOCAL, ENC_D)
    grad_normed = grad * gain_ref[...]
    grad_mixed = inverse * (
        grad_normed - normed * jnp.mean(grad_normed * normed, axis=-1, keepdims=True)
    )
    grad_low = low(grad_mixed)
    low_loc[...] = grad_low.reshape(NSET, LOCAL, ENC_D)
    low_copies = []
    for i, peer in enumerate(sec):
        copy = remote(
            low_loc, low_all.at[:, row_slot(me), :], low_send.at[i], low_rsem.at[i], peer
        )
        copy.start()
        low_copies.append(copy)
    gain_row = jnp.sum(grad * normed, axis=0, keepdims=True)
    gain_loc[...] = jnp.concatenate(
        [gain_row[:, i * 128 : (i + 1) * 128] for i in range(7)]
        + [jnp.zeros((1, 128), jnp.float32)],
        axis=0,
    )
    for i, peer in enumerate(sec):
        copy = remote(gain_loc, gain_all.at[i], gn_send.at[i], gn_rsem.at[i], peer)
        copy.start()
        low_copies.append(copy)
    low_all[:, row_slot(me), :] = low_loc[...]
    embed = grad_mixed + dot_nt(grad_low, encw_ref[...])
    eg_ref[...] = low(embed).reshape(NSET, LOCAL, ENC_D)

    y_copy.wait_recv()
    kvg_ref[...] = f32(fin_ref[yhi]) + f32(y_recv[...])

    for copy in low_copies:
        copy.wait_recv()
    weight = dot_nn(
        xt_ref[pl.ds(pl.multiple_of(me * OWN_ROWS, 16), OWN_ROWS), :],
        low_all[...].reshape(ROWS, ENC_D),
    )
    gain_sum = gain_loc[...]
    for i in range(N_SEC - 1):
        gain_sum = gain_sum + gain_all[i]
    weight = jnp.concatenate([weight, jnp.zeros((OWN_ROWS, 128), jnp.float32)], axis=1)
    for j in range(4):
        wp_ref[j, 0 : N_Z - 1] = low(weight[:, j * QUAD_COLS : (j + 1) * QUAD_COLS]).reshape(
            N_Z - 1, PIECE, QUAD_COLS
        )
        extra = jnp.zeros((PIECE, QUAD_COLS), jnp.float32)
        if j == 0:
            extra = jnp.concatenate(
                [
                    jnp.concatenate([gain_sum, jnp.zeros((8, 128), jnp.float32)], axis=1),
                    jnp.zeros((8, QUAD_COLS), jnp.float32),
                ],
                axis=0,
            )
        wp_ref[j, N_Z - 1] = low(extra)
    my_quad = yhi * 2 + core
    quad_ids = [yhi * 2 + (1 - core), (1 - yhi) * 2 + core, (1 - yhi) * 2 + (1 - core)]
    quad_copies = []
    for i in range(3):
        copy = remote(
            wp_ref.at[quad_ids[i]], quad_recv.at[i], quad_send.at[i], quad_rsem.at[i], quad[i]
        )
        copy.start()
        quad_copies.append(copy)
    for copy in quad_copies:
        copy.wait_recv()
    zp_ref[...] = low(
        f32(wp_ref[my_quad]) + f32(quad_recv[0]) + f32(quad_recv[1]) + f32(quad_recv[2])
    )
    z_copies = []
    for i, peer in enumerate(z_peers):
        copy = remote(
            zp_ref.at[lax.rem(zed + i + 1, N_Z)], z_recv.at[i], z_send.at[i], z_rsem.at[i], peer
        )
        copy.start()
        z_copies.append(copy)
    total = f32(zp_ref[zed])
    for i in range(N_Z - 1):
        z_copies[i].wait_recv()
        total = total + f32(z_recv[i])
    za_ref[...] = low(total)
    za_copies = []
    for i, peer in enumerate(z_peers):
        copy = remote(za_ref, za_all.at[zed], za_send.at[i], za_rsem.at[i], peer)
        copy.start()
        za_copies.append(copy)
    za_all[zed] = za_ref[...]
    for copy in za_copies:
        copy.wait_recv()
    wa_copies = []
    for i in range(3):
        copy = remote(za_all, wa_all.at[my_quad], wa_send.at[i], wa_rsem.at[i], quad[i])
        copy.start()
        wa_copies.append(copy)
    wa_all[my_quad] = za_all[...]

    y_copy.wait_send()
    for group in (x_copies, sec_copies, low_copies, quad_copies, z_copies, za_copies):
        for copy in group:
            copy.wait_send()
    for i in range(N_Z):
        core_copy(i).wait_send()
    for s in range(4):
        for copy in ring_copies(s):
            copy.wait_send()

    for copy in wa_copies:
        copy.wait_recv()
    for j in range(4):
        width = min(QUAD_COLS, ENC_D - j * QUAD_COLS)
        wg_ref[:, j * QUAD_COLS : j * QUAD_COLS + width] = f32(
            wa_all[j, 0 : N_Z - 1].reshape(OWN_ROWS, QUAD_COLS)[:, :width]
        )
    gg_ref[...] = f32(wa_all[0, N_Z - 1])[:8, :128]
    for copy in wa_copies:
        copy.wait_send()


def train(ids, x_local, gain, enc_weight, kv_weight, queries, pos_bias, ctx_grad):
    bf, fl = jnp.bfloat16, jnp.float32
    dma = pltpu.SemaphoreType.DMA
    vmem = pltpu.VMEM
    any_spec = pl.BlockSpec(memory_space=pl.ANY)
    width = HEADS * HEAD
    return pl.pallas_call(
        train_kernel,
        out_shape=[
            jax.ShapeDtypeStruct((1, TOK_DEV, width), bf),
            jax.ShapeDtypeStruct((HEAD, ENC_D), fl),
            jax.ShapeDtypeStruct((OWN_ROWS, ENC_D), fl),
            jax.ShapeDtypeStruct((8, 128), fl),
            jax.ShapeDtypeStruct((NSET, LOCAL, ENC_D), bf),
        ],
        in_specs=[VMEM_SPEC] * 3 + [any_spec] * 5,
        out_specs=[VMEM_SPEC] * 5,
        scratch_shapes=[
            vmem((ENC_D, ENC_D), bf),
            vmem((2 * width, ENC_D), bf),
            vmem((TOK_DEV, width), bf),
            vmem((HEADS, BLOCK, NBR * NLEN), bf),
            vmem((TOK_DEV, width), bf),
            vmem((NSET, NLEN, ENC_D), bf),
            vmem((NSET, NLEN, ENC_D), bf),
            vmem((ENC_D, ROWS), bf),
            vmem((ROWS, 2 * width), bf),
            vmem((2, N_Z, 2, HEAD, ENC_D), bf),
            vmem((N_Z, 2, HEAD, ENC_D), bf),
            vmem((2, HEAD, ENC_D), bf),
            vmem((4, 2, HEAD, ENC_D), bf),
            vmem((4, 2, HEAD, ENC_D), bf),
            vmem((2, HEAD, ENC_D), bf),
            vmem((HEAD, ENC_D), bf),
            vmem((NSET, NLEN, ENC_D), bf),
            vmem((N_SEC - 1, NSET, LOCAL, ENC_D), bf),
            vmem((NSET, NLEN, ENC_D), bf),
            vmem((NSET, LOCAL, ENC_D), bf),
            vmem((N_SEC - 1, 8, 128), fl),
            vmem((8, 128), fl),
            vmem((4, N_Z, PIECE, QUAD_COLS), bf),
            vmem((3, N_Z, PIECE, QUAD_COLS), bf),
            vmem((N_Z, PIECE, QUAD_COLS), bf),
            vmem((N_Z - 1, PIECE, QUAD_COLS), bf),
            vmem((PIECE, QUAD_COLS), bf),
            vmem((N_Z, PIECE, QUAD_COLS), bf),
            vmem((4, N_Z, PIECE, QUAD_COLS), bf),
            dma((5,)),
            dma((7,)),
            dma((7,)),
            dma((8,)),
            dma((8,)),
            dma((4, 2)),
            dma((4, 2)),
            dma,
            dma,
            dma((2, 7)),
            dma((2, 7)),
            dma((7,)),
            dma((7,)),
            dma((7,)),
            dma((7,)),
            dma((3,)),
            dma((3,)),
            dma((7,)),
            dma((7,)),
            dma((7,)),
            dma((7,)),
            dma((3,)),
            dma((3,)),
        ],
        compiler_params=pltpu.CompilerParams(
            collective_id=0, has_side_effects=True, vmem_limit_bytes=62 * 1024 * 1024
        ),
        name="train",
    )(ids, x_local, gain, enc_weight, kv_weight, queries, pos_bias, ctx_grad)


def finish_kernel(q_in, k_in, w_in, g_in, e_in, q_out, k_out, w_out, g_out, e_out):
    q_out[...] = q_in[...]
    k_out[...] = k_in[...]
    w_out[...] = w_in[...]
    for i in range(7):
        g_out[:, i * 128 : (i + 1) * 128] = g_in[i : i + 1, :]
    e_out[...] = e_in[...]


def finish(outs):
    shapes = [jax.ShapeDtypeStruct(o.shape, o.dtype) for o in outs]
    shapes[3] = jax.ShapeDtypeStruct((1, ENC_D), jnp.float32)
    return pl.pallas_call(
        finish_kernel,
        out_shape=shapes,
        in_specs=[VMEM_SPEC] * 5,
        out_specs=[VMEM_SPEC] * 5,
        name="finish",
    )(*outs)


def body(nbr_embed, enc_weight, enc_gain, kv_weight, queries, pos_bias, nbr_ids, ctx_grad):
    outs = train(
        jnp.repeat(nbr_ids[0].T, BLOCK, axis=1),
        nbr_embed[0],
        enc_gain[None, :],
        enc_weight,
        kv_weight,
        queries,
        pos_bias,
        ctx_grad,
    )
    q_grad, kv_grad, w_grad, g_grad, e_grad = finish(outs)
    return (q_grad, kv_grad[None], w_grad, g_grad.reshape(ENC_D), e_grad[None])


def solution(mesh):
    return jax.shard_map(
        body,
        mesh=mesh,
        in_specs=(
            P("dp", None, "section", None),
            P(),
            P(),
            P("section", None, None),
            P("section", "dp", None),
            P("section", None, None, None),
            P("dp", None, None),
            P("section", "dp", None),
        ),
        out_specs=(
            P("section", "dp", None),
            P("section", "dp", None),
            P("section", None),
            P(),
            P("dp", None, "section", None),
        ),
        check_vma=False,
    )
```

```python
import math

import jax
import jax.numpy as jnp
from jax import lax
from jax.experimental import pallas as pl
from jax.experimental.pallas import tpu as pltpu
from jax.sharding import PartitionSpec as P

HEADS = 16
HEAD = 128
ENC_D = 896
BLOCK = 64
NBR = 2
NLEN = 128
TOK_DEV = 128
NSET = 4
ROWS = NSET * NLEN
N_SEC = 8
N_Z = 8
LOCAL = NLEN // N_SEC
OWN_ROWS = ENC_D // N_SEC
PIECE = 16
QUAD_COLS = 256
FACTOR = 1.0 / math.sqrt(HEAD)
MESH = pl.DeviceIdType.MESH

eps_norm = 1e-06

VMEM_SPEC = pl.BlockSpec(memory_space=pltpu.VMEM)


def greet(peers):
    barrier = pltpu.get_barrier_semaphore()
    for peer in peers:
        pl.semaphore_signal(barrier, inc=1, device_id=peer, device_id_type=MESH)
    pl.semaphore_wait(barrier, len(peers))


def remote(src, dst, send_sem, recv_sem, peer):
    return pltpu.make_async_remote_copy(
        src_ref=src,
        dst_ref=dst,
        send_sem=send_sem,
        recv_sem=recv_sem,
        device_id=peer,
        device_id_type=MESH,
    )


def section_ids(me):
    y, x = me // 4, lax.rem(me, 4)
    steps = [(1, 0), (0, 1), (0, 3), (1, 1), (1, 3), (0, 2), (1, 2)]
    return [lax.rem(y + a, 2) * 4 + lax.rem(x + b, 4) for a, b in steps]


def section_sources(me):
    y, x = me // 4, lax.rem(me, 4)
    steps = [(1, 0), (0, 3), (0, 1), (1, 3), (1, 1), (0, 2), (1, 2)]
    return [lax.rem(y + a, 2) * 4 + lax.rem(x + b, 4) for a, b in steps]


def row_slot(index):
    return pl.ds(pl.multiple_of(index * LOCAL, LOCAL), LOCAL)


def dot_nt(a, b):
    return lax.dot_general(a, b, (((1,), (1,)), ((), ())), preferred_element_type=jnp.float32)


def dot_tn(a, b):
    return lax.dot_general(a, b, (((0,), (0,)), ((), ())), preferred_element_type=jnp.float32)


def dot_nn(a, b):
    return jnp.dot(a, b, preferred_element_type=jnp.float32)


def encode(x, enc_weight):
    mixed = x.astype(jnp.float32) + dot_nn(x, enc_weight)
    inverse = lax.rsqrt(jnp.mean(mixed * mixed, axis=-1, keepdims=True) + eps_norm)
    return mixed * inverse, inverse


def f32(x):
    return x.astype(jnp.float32)


def low(x):
    return x.astype(jnp.bfloat16)


def train_kernel(
    ids_ref,
    x_ref,
    gain_ref,
    encw_hbm,
    w_hbm,
    q_hbm,
    bias_hbm,
    g_hbm,
    qg_ref,
    kvg_ref,
    wg_ref,
    gg_ref,
    eg_ref,
    encw_ref,
    w_ref,
    q_ref,
    bias_ref,
    g_ref,
    x_all,
    enc_ref,
    xt_ref,
    gs_ref,
    dw_ref,
    core_recv,
    first_ref,
    plus_recv,
    minus_recv,
    fin_ref,
    y_recv,
    de_ref,
    de_recv,
    low_all,
    low_loc,
    gain_all,
    gain_loc,
    wp_ref,
    quad_recv,
    zp_ref,
    z_recv,
    za_ref,
    za_all,
    wa_all,
    load_sem,
    x_send,
    x_rsem,
    core_send,
    core_rsem,
    ring_send,
    ring_rsem,
    y_send,
    y_rsem,
    sec_send,
    sec_rsem,
    low_send,
    low_rsem,
    gn_send,
    gn_rsem,
    quad_send,
    quad_rsem,
    z_send,
    z_rsem,
    za_send,
    za_rsem,
    wa_send,
    wa_rsem,
):
    me = lax.axis_index("section")
    dp = lax.axis_index("dp")
    core = lax.rem(dp, 2)
    zed = lax.rem(dp // 2, N_Z)
    yhi = dp // (2 * N_Z)

    gain = gain_ref[...].reshape(1, ENC_D)
    loads = [
        pltpu.make_async_copy(encw_hbm, encw_ref, load_sem.at[0]),
        pltpu.make_async_copy(w_hbm.at[0], w_ref, load_sem.at[1]),
        pltpu.make_async_copy(q_hbm.at[0], q_ref, load_sem.at[2]),
        pltpu.make_async_copy(bias_hbm.at[0], bias_ref, load_sem.at[3]),
        pltpu.make_async_copy(g_hbm.at[0], g_ref, load_sem.at[4]),
    ]
    for copy in loads:
        copy.start()

    def dp_peer(y, z, c):
        return {"dp": (y * N_Z + z) * 2 + c}

    targets = section_ids(me)
    sources = section_sources(me)
    sec = [{"section": t} for t in targets]
    z_peers = [dp_peer(yhi, lax.rem(zed + d, N_Z), core) for d in range(1, N_Z)]
    z_next, z_prev = z_peers[0], z_peers[N_Z - 2]
    core_peer = dp_peer(yhi, zed, 1 - core)
    y_peer = dp_peer(1 - yhi, zed, core)
    quad = [core_peer, y_peer, dp_peer(1 - yhi, zed, 1 - core)]
    greet(sec + z_peers + quad)

    x_copies = []
    for i, peer in enumerate(sec):
        copy = remote(x_ref, x_all.at[:, row_slot(me), :], x_send.at[i], x_rsem.at[i], peer)
        copy.start()
        x_copies.append(copy)
    x_all[:, row_slot(me), :] = x_ref[...]
    loads[0].wait()

    def encode_slots(slots):
        x = jnp.concatenate(
            [x_all[:, row_slot(s), :].reshape(NSET * LOCAL, ENC_D) for s in slots], axis=0
        )
        normed, _ = encode(x, encw_ref[...])
        encoded = low(normed * gain)
        for n, s in enumerate(slots):
            enc_ref[:, row_slot(s), :] = encoded[
                n * NSET * LOCAL : (n + 1) * NSET * LOCAL
            ].reshape(NSET, LOCAL, ENC_D)

    for i in range(3):
        x_copies[i].wait_recv()
    encode_slots([me] + sources[:3])
    for i in range(3, 7):
        x_copies[i].wait_recv()
    encode_slots(sources[3:])
    for copy in loads[1:]:
        copy.wait()

    front = lax.broadcasted_iota(jnp.int32, (1, TOK_DEV), 1) < BLOCK
    idm = ids_ref[0]
    marks = [jnp.where(front, idm[0:1, n : n + 1], idm[1:2, n : n + 1]) for n in range(NBR)]
    hits = [[marks[n] == e for e in range(NSET)] for n in range(NBR)]

    def picked(n, parts):
        chosen = parts[NSET - 1]
        for e in range(NSET - 2, -1, -1):
            chosen = jnp.where(hits[n][e], parts[e], chosen)
        return chosen

    def core_z(i):
        half = (i + 1) // 2
        return lax.rem(zed + 4 + half * (1 - 2 * lax.rem(i, 2)), N_Z)

    def core_copy(i):
        z = core_z(i)
        return remote(
            dw_ref.at[1 - core, z], core_recv.at[z], core_send.at[i], core_rsem.at[i], core_peer
        )

    def chip_sum(z, y):
        return f32(dw_ref[core, z, y]) + f32(core_recv[z, y])

    streams = ((plus_recv, z_next, -1), (minus_recv, z_prev, 1))

    def ring_copy(d, stream, hop):
        recv, peer, _ = streams[d]
        y = d if stream == 0 else 1 - d
        start = 0 if stream == 0 else 1
        src = first_ref.at[d, stream] if hop == start else recv.at[hop - 1, y]
        return remote(
            src, recv.at[hop, y], ring_send.at[d, stream, hop], ring_rsem.at[d, stream, hop], peer
        )

    def ring_step(stream, hop):
        start = 0 if stream == 0 else 1
        for d in range(2):
            recv, _, sign = streams[d]
            y = d if stream == 0 else 1 - d
            z = lax.rem(zed + 4 + sign * hop, N_Z)
            if stream == 1:
                core_copy(2 * hop - 1 + d).wait_recv()
            elif hop == 0 and d == 0:
                core_copy(0).wait_recv()
            if hop == start:
                first_ref[d, stream] = low(chip_sum(z, y))
            else:
                ring_copy(d, stream, hop - 1).wait_recv()
                recv[hop - 1, y] = low(chip_sum(z, y) + f32(recv[hop - 1, y]))
            ring_copy(d, stream, hop).start()

    def pair(i, carry):
        z = core_z(i)
        cols = pl.ds(pl.multiple_of(z * 2 * HEAD, 2 * HEAD), 2 * HEAD)
        vcols = pl.ds(
            pl.multiple_of(HEADS * HEAD + z * 2 * HEAD, 2 * HEAD), 2 * HEAD
        )
        enc = enc_ref[...].reshape(ROWS, ENC_D)
        keys = low(dot_nt(enc, w_ref[cols, :]))
        vals = low(dot_nt(enc, w_ref[vcols, :]))
        q2, g2 = q_ref[:, cols], g_ref[:, cols]
        dks, dvs, dkts, dvts, dqs = [], [], [], [], []
        heads = []
        for a in range(2):
            span = slice(a * HEAD, (a + 1) * HEAD)
            s_all = dot_nt(keys[:, span], q2[:, span])
            dp_all = dot_nt(vals[:, span], g2[:, span])
            b = f32(bias_ref[2 * z + a])
            heads.append((jnp.concatenate([b, b], axis=0).T, span, s_all, dp_all))
        for bias, span, s_all, dp_all in heads:
            q, g, k = q2[:, span], g2[:, span], keys[:, span]
            s_sets = [s_all[e * NLEN : (e + 1) * NLEN] for e in range(NSET)]
            dp_sets = [dp_all[e * NLEN : (e + 1) * NLEN] for e in range(NSET)]
            scores = [
                picked(n, s_sets) * FACTOR + bias[n * NLEN : (n + 1) * NLEN]
                for n in range(NBR)
            ]
            dprobs = [picked(n, dp_sets) for n in range(NBR)]
            peak = jnp.max(jnp.maximum(scores[0], scores[1]), axis=0, keepdims=True)
            ex = [jnp.exp(s - peak) for s in scores]
            share = 1.0 / jnp.sum(ex[0] + ex[1], axis=0, keepdims=True)
            p = [e * share for e in ex]
            inner = jnp.sum(p[0] * dprobs[0] + p[1] * dprobs[1], axis=0, keepdims=True)
            ds = [f32(low(p[n] * (dprobs[n] - inner))) for n in range(NBR)]
            pb = [f32(low(p[n])) for n in range(NBR)]
            zero = jnp.zeros_like(ds[0])
            ds_t, p_t = [], []
            for e in range(NSET):
                hit = [hits[n][e] for n in range(NBR)]
                ds_t.append(low(jnp.where(hit[0], ds[0], zero) + jnp.where(hit[1], ds[1], zero)))
                p_t.append(low(jnp.where(hit[0], pb[0], zero) + jnp.where(hit[1], pb[1], zero)))
            ds_t = jnp.concatenate(ds_t, axis=0)
            p_t = jnp.concatenate(p_t, axis=0)
            dks.append(low(dot_nn(ds_t, q) * FACTOR))
            dvs.append(low(dot_nn(p_t, g)))
            dkts.append(low(dot_nt(q.T, ds_t) * FACTOR))
            dvts.append(low(dot_nt(g.T, p_t)))
            dqs.append(low(dot_tn(ds_t, k) * FACTOR))
        qg_ref[0, :, cols] = jnp.concatenate(dqs, axis=1)
        gs_ref[:, cols] = jnp.concatenate(dks, axis=1)
        gs_ref[:, vcols] = jnp.concatenate(dvs, axis=1)
        dw = low(dot_nn(jnp.concatenate(dkts + dvts, axis=0), enc))
        for y in range(2):
            for c in range(2):
                at = (2 * y + c) * HEAD
                dw_ref[c, z, y] = dw[at : at + HEAD]
        core_copy(i).start()
        for at, stream, hop in ((1, 0, 0), (3, 1, 1), (5, 0, 1)):

            @pl.when(i == at)
            def _(stream=stream, hop=hop):
                ring_step(stream, hop)

        return carry

    lax.fori_loop(0, N_Z, pair, 0)
    ring_step(1, 2)

    sec_copies = [[], []]
    for half in range(2):
        rows = pl.ds(half * 2 * NLEN, 2 * NLEN)
        two = slice(2 * half, 2 * half + 2)
        de_ref[two] = low(dot_nn(gs_ref[rows, :], w_ref[...])).reshape(2, NLEN, ENC_D)
        for i, peer in enumerate(sec):
            copy = remote(
                de_ref.at[two, row_slot(targets[i]), :],
                de_recv.at[i, two],
                sec_send.at[half, i],
                sec_rsem.at[half, i],
                peer,
            )
            copy.start()
            sec_copies[half].append(copy)

    normed_rows, inverse_rows = encode(x_ref[...].reshape(NSET * LOCAL, ENC_D), encw_ref[...])
    xt_ref[...] = x_all[...].reshape(ROWS, ENC_D).T
    ring_step(0, 2)

    low_copies = [[], []]
    mixed_parts, low_parts = [], []
    gain_row = jnp.zeros((1, ENC_D), jnp.float32)
    for half in range(2):
        two = slice(2 * half, 2 * half + 2)
        own = slice(2 * LOCAL * half, 2 * LOCAL * (half + 1))
        normed, inverse = normed_rows[own], inverse_rows[own]
        for copy in sec_copies[half]:
            copy.wait_recv()
        grad = f32(de_ref[two, row_slot(me), :])
        for i in range(N_SEC - 1):
            grad = grad + f32(de_recv[i, two])
        grad = grad.reshape(2 * LOCAL, ENC_D)
        grad_normed = grad * gain
        grad_mixed = inverse * (
            grad_normed - normed * jnp.mean(grad_normed * normed, axis=-1, keepdims=True)
        )
        grad_low = low(grad_mixed)
        low_loc[two] = grad_low.reshape(2, LOCAL, ENC_D)
        for i, peer in enumerate(sec):
            copy = remote(
                low_loc.at[two],
                low_all.at[two, row_slot(me), :],
                low_send.at[half, i],
                low_rsem.at[half, i],
                peer,
            )
            copy.start()
            low_copies[half].append(copy)
        low_all[two, row_slot(me), :] = low_loc[two]
        gain_row = gain_row + jnp.sum(grad * normed, axis=0, keepdims=True)
        mixed_parts.append(grad_mixed)
        low_parts.append(grad_low)
    gain_loc[...] = jnp.concatenate(
        [gain_row[:, i * 128 : (i + 1) * 128] for i in range(7)]
        + [jnp.zeros((1, 128), jnp.float32)],
        axis=0,
    )
    gain_copies = []
    for i, peer in enumerate(sec):
        copy = remote(gain_loc, gain_all.at[i], gn_send.at[i], gn_rsem.at[i], peer)
        copy.start()
        gain_copies.append(copy)
    embed = jnp.concatenate(mixed_parts, axis=0) + dot_nt(
        jnp.concatenate(low_parts, axis=0), encw_ref[...]
    )
    eg_ref[...] = low(embed).reshape(NSET, LOCAL, ENC_D)
    ring_step(1, 3)

    mine = pl.ds(pl.multiple_of(me * OWN_ROWS, 16), OWN_ROWS)
    weight = None
    for half in range(2):
        two = slice(2 * half, 2 * half + 2)
        for copy in low_copies[half]:
            copy.wait_recv()
        part = dot_nn(
            xt_ref[mine, 2 * NLEN * half : 2 * NLEN * (half + 1)],
            low_all[two].reshape(2 * NLEN, ENC_D),
        )
        weight = part if half == 0 else weight + part
        if half == 0:
            ring_step(0, 3)
    for copy in gain_copies:
        copy.wait_recv()
    gain_sum = gain_loc[...]
    for i in range(N_SEC - 1):
        gain_sum = gain_sum + gain_all[i]
    weight = jnp.concatenate([weight, jnp.zeros((OWN_ROWS, 128), jnp.float32)], axis=1)
    for j in range(4):
        wp_ref[j, 0 : N_Z - 1] = low(weight[:, j * QUAD_COLS : (j + 1) * QUAD_COLS]).reshape(
            N_Z - 1, PIECE, QUAD_COLS
        )
        extra = jnp.zeros((PIECE, QUAD_COLS), jnp.float32)
        if j == 0:
            extra = jnp.concatenate(
                [
                    jnp.concatenate([gain_sum, jnp.zeros((8, 128), jnp.float32)], axis=1),
                    jnp.zeros((8, QUAD_COLS), jnp.float32),
                ],
                axis=0,
            )
        wp_ref[j, N_Z - 1] = low(extra)
    my_quad = yhi * 2 + core
    quad_ids = [yhi * 2 + (1 - core), (1 - yhi) * 2 + core, (1 - yhi) * 2 + (1 - core)]
    quad_copies = []
    for i in range(3):
        copy = remote(
            wp_ref.at[quad_ids[i]], quad_recv.at[i], quad_send.at[i], quad_rsem.at[i], quad[i]
        )
        copy.start()
        quad_copies.append(copy)
    for copy in quad_copies:
        copy.wait_recv()
    zp_ref[...] = low(
        f32(wp_ref[my_quad]) + f32(quad_recv[0]) + f32(quad_recv[1]) + f32(quad_recv[2])
    )
    z_copies = []
    for i, peer in enumerate(z_peers):
        copy = remote(
            zp_ref.at[lax.rem(zed + i + 1, N_Z)], z_recv.at[i], z_send.at[i], z_rsem.at[i], peer
        )
        copy.start()
        z_copies.append(copy)
    core_copy(N_Z - 1).wait_recv()
    for d in range(2):
        for stream in range(2):
            ring_copy(d, stream, 3).wait_recv()
    for y in range(2):
        fin_ref[y] = low(chip_sum(zed, y) + f32(plus_recv[3, y]) + f32(minus_recv[3, y]))
    y_copy = remote(fin_ref.at[1 - yhi], y_recv, y_send, y_rsem, y_peer)
    y_copy.start()
    total = f32(zp_ref[zed])
    for i in range(N_Z - 1):
        z_copies[i].wait_recv()
        total = total + f32(z_recv[i])
    za_ref[...] = low(total)
    za_copies = []
    for i, peer in enumerate(z_peers):
        copy = remote(za_ref, za_all.at[zed], za_send.at[i], za_rsem.at[i], peer)
        copy.start()
        za_copies.append(copy)
    za_all[zed] = za_ref[...]
    y_copy.wait_recv()
    kvg_ref[...] = f32(fin_ref[yhi]) + f32(y_recv[...])
    for copy in za_copies:
        copy.wait_recv()
    wa_copies = []
    for i in range(3):
        copy = remote(za_all, wa_all.at[my_quad], wa_send.at[i], wa_rsem.at[i], quad[i])
        copy.start()
        wa_copies.append(copy)
    wa_all[my_quad] = za_all[...]

    y_copy.wait_send()
    for group in [x_copies, gain_copies, quad_copies, z_copies, za_copies] + (
        sec_copies + low_copies
    ):
        for copy in group:
            copy.wait_send()
    for i in range(N_Z):
        core_copy(i).wait_send()
    for d in range(2):
        for hop in range(4):
            ring_copy(d, 0, hop).wait_send()
            if hop > 0:
                ring_copy(d, 1, hop).wait_send()

    for copy in wa_copies:
        copy.wait_recv()
    for j in range(4):
        width = min(QUAD_COLS, ENC_D - j * QUAD_COLS)
        wg_ref[:, j * QUAD_COLS : j * QUAD_COLS + width] = f32(
            wa_all[j, 0 : N_Z - 1].reshape(OWN_ROWS, QUAD_COLS)[:, :width]
        )
    gg_ref[...] = f32(wa_all[0, N_Z - 1])[:8, :128]
    for copy in wa_copies:
        copy.wait_send()


def train(ids, x_local, gain, enc_weight, kv_weight, queries, pos_bias, ctx_grad):
    bf, fl = jnp.bfloat16, jnp.float32
    dma = pltpu.SemaphoreType.DMA
    vmem = pltpu.VMEM
    any_spec = pl.BlockSpec(memory_space=pl.ANY)
    width = HEADS * HEAD
    return pl.pallas_call(
        train_kernel,
        out_shape=[
            jax.ShapeDtypeStruct((1, TOK_DEV, width), bf),
            jax.ShapeDtypeStruct((HEAD, ENC_D), fl),
            jax.ShapeDtypeStruct((OWN_ROWS, ENC_D), fl),
            jax.ShapeDtypeStruct((8, 128), fl),
            jax.ShapeDtypeStruct((NSET, LOCAL, ENC_D), bf),
        ],
        in_specs=[VMEM_SPEC] * 3 + [any_spec] * 5,
        out_specs=[VMEM_SPEC] * 5,
        scratch_shapes=[
            vmem((ENC_D, ENC_D), bf),
            vmem((2 * width, ENC_D), bf),
            vmem((TOK_DEV, width), bf),
            vmem((HEADS, BLOCK, NBR * NLEN), bf),
            vmem((TOK_DEV, width), bf),
            vmem((NSET, NLEN, ENC_D), bf),
            vmem((NSET, NLEN, ENC_D), bf),
            vmem((ENC_D, ROWS), bf),
            vmem((ROWS, 2 * width), bf),
            vmem((2, N_Z, 2, HEAD, ENC_D), bf),
            vmem((N_Z, 2, HEAD, ENC_D), bf),
            vmem((2, 2, HEAD, ENC_D), bf),
            vmem((4, 2, HEAD, ENC_D), bf),
            vmem((4, 2, HEAD, ENC_D), bf),
            vmem((2, HEAD, ENC_D), bf),
            vmem((HEAD, ENC_D), bf),
            vmem((NSET, NLEN, ENC_D), bf),
            vmem((N_SEC - 1, NSET, LOCAL, ENC_D), bf),
            vmem((NSET, NLEN, ENC_D), bf),
            vmem((NSET, LOCAL, ENC_D), bf),
            vmem((N_SEC - 1, 8, 128), fl),
            vmem((8, 128), fl),
            vmem((4, N_Z, PIECE, QUAD_COLS), bf),
            vmem((3, N_Z, PIECE, QUAD_COLS), bf),
            vmem((N_Z, PIECE, QUAD_COLS), bf),
            vmem((N_Z - 1, PIECE, QUAD_COLS), bf),
            vmem((PIECE, QUAD_COLS), bf),
            vmem((N_Z, PIECE, QUAD_COLS), bf),
            vmem((4, N_Z, PIECE, QUAD_COLS), bf),
            dma((5,)),
            dma((7,)),
            dma((7,)),
            dma((8,)),
            dma((8,)),
            dma((2, 2, 4)),
            dma((2, 2, 4)),
            dma,
            dma,
            dma((2, 7)),
            dma((2, 7)),
            dma((2, 7)),
            dma((2, 7)),
            dma((7,)),
            dma((7,)),
            dma((3,)),
            dma((3,)),
            dma((7,)),
            dma((7,)),
            dma((7,)),
            dma((7,)),
            dma((3,)),
            dma((3,)),
        ],
        compiler_params=pltpu.CompilerParams(
            collective_id=0, has_side_effects=True, vmem_limit_bytes=62 * 1024 * 1024
        ),
        name="train",
    )(ids, x_local, gain, enc_weight, kv_weight, queries, pos_bias, ctx_grad)


def finish_kernel(*refs):
    ins, outs, holds = refs[:4], refs[5:9], refs[10:14]
    g_in, g_out = refs[4], refs[9]
    in_sem, out_sem = refs[14], refs[15]
    fetch = [
        pltpu.make_async_copy(a, b, in_sem.at[i]) for i, (a, b) in enumerate(zip(ins, holds))
    ]
    store = [
        pltpu.make_async_copy(a, b, out_sem.at[i]) for i, (a, b) in enumerate(zip(holds, outs))
    ]
    for copy in fetch:
        copy.start()
    for i in range(7):
        g_out[i * 128 : (i + 1) * 128] = g_in[i]
    for a, b in zip(fetch, store):
        a.wait()
        b.start()
    for copy in store:
        copy.wait()


def finish(q_grad, kv_grad, w_grad, g_grad, e_grad):
    bulk = [q_grad, kv_grad, w_grad, e_grad]
    any_spec = pl.BlockSpec(memory_space=pl.ANY)
    return pl.pallas_call(
        finish_kernel,
        out_shape=[jax.ShapeDtypeStruct(o.shape, o.dtype) for o in bulk]
        + [jax.ShapeDtypeStruct((ENC_D,), jnp.float32)],
        in_specs=[any_spec] * 4 + [VMEM_SPEC],
        out_specs=[any_spec] * 4 + [VMEM_SPEC],
        scratch_shapes=[pltpu.VMEM(o.shape, o.dtype) for o in bulk]
        + [pltpu.SemaphoreType.DMA((4,)), pltpu.SemaphoreType.DMA((4,))],
        compiler_params=pltpu.CompilerParams(vmem_limit_bytes=62 * 1024 * 1024),
        name="finish",
    )(*bulk, g_grad)


def body(nbr_embed, enc_weight, enc_gain, kv_weight, queries, pos_bias, nbr_ids, ctx_grad):
    outs = train(
        nbr_ids,
        nbr_embed[0],
        enc_gain,
        enc_weight,
        kv_weight,
        queries,
        pos_bias,
        ctx_grad,
    )
    q_grad, kv_grad, w_grad, e_grad, g_grad = finish(*outs)
    return (q_grad, kv_grad[None], w_grad, g_grad, e_grad[None])


def solution(mesh):
    return jax.shard_map(
        body,
        mesh=mesh,
        in_specs=(
            P("dp", None, "section", None),
            P(),
            P(),
            P("section", None, None),
            P("section", "dp", None),
            P("section", None, None, None),
            P("dp", None, None),
            P("section", "dp", None),
        ),
        out_specs=(
            P("section", "dp", None),
            P("section", "dp", None),
            P("section", None),
            P(),
            P("dp", None, "section", None),
        ),
        check_vma=False,
    )
```
